256 devices in a mesh: dp: 32 (over z, y_hi, core), expert: 8 (over x, y_lo).
Axes of the slice: x: 4, y: 4 (y_hi: 2, y_lo: 2; y = y_hi * 2 + y_lo), z: 8, core: 2. Of those that a mesh axis runs over, the one named last changes fastest.
Arguments:
- tokens: bfloat16 [32768, 2048], P(('dp', 'expert')), may hold values from -24 to 24
- cotangent: bfloat16 [32768, 2048], P(('dp', 'expert')), may hold values from -24 to 24
- expert_ids: int32 [32768, 2], P(('dp', 'expert')), may hold values from 0 to 7, all different within a row; in each aligned block of 128 rows (0 to 127, 128 to 255, ...) at most 40 rows name the same one
- gate_weights: float32 [32768, 2], P(('dp', 'expert')), may hold values from 0.1 to 1
- partner: int32 [8], replicated, may hold values from 0 to 7, as said below
- w_gate: bfloat16 [8, 2048, 768], P('expert'), may hold values from -0.125 to 0.125
- w_up: bfloat16 [8, 2048, 768], P('expert'), may hold values from -0.125 to 0.125
- w_down: bfloat16 [8, 768, 2048], P('expert'), may hold values from -0.21875 to 0.21875
Outputs:
- mixed_out: bfloat16 [32768, 2048], P(('dp', 'expert'))
- token_grad: bfloat16 [32768, 2048], P(('dp', 'expert'))
- gate_grad: float32 [32768, 2], P(('dp', 'expert'))
- slot_grad_gate: float32 [8, 2048, 768], P('expert', 'dp')
- slot_grad_up: float32 [8, 2048, 768], P('expert', 'dp')
- slot_grad_down: float32 [8, 768, 2048], P('expert', None, 'dp')
The draws below stay inside these ranges and needn't reach their ends.
Inputs may be any that keep to these rules, and one draw needn't show every extreme that they name: `expert_ids`: each row names 2 different experts. Among the 128 rows of one device no expert is named by more than 40 rows, and in every draw some device names some expert exactly 40 times. partner[partner[i]] = i and partner[i] != i for every slot i.
All inputs are finite; a program needn't handle non-finite values.
Results may differ from the reference program's by a relative error of at most 0.015.
Values may be sent and summed in bfloat16 or wider, within the bound.
A program may use at most 128 MiB of HBM per device.

```python
import math
import jax
import jax.numpy as jnp
import numpy as np
from jax import lax

D = 2048
FF = 768
TOPK = 2
TOK_DEV = 128
EXPERTS = 8
CAP = 40
TOKENS = 32768
N_DP = 32


def draw_partner(key, part):
    order = jax.random.permutation(key, EXPERTS).astype(jnp.int32)
    positions = jnp.arange(EXPERTS, dtype=jnp.int32)
    mates = order[positions ^ 1]
    return jnp.zeros((EXPERTS,), jnp.int32).at[order].set(mates)


def strengthened(values, rng, source, target, shards_of, factor):
    def block_of(dim):
        return (jnp.arange(values.shape[dim]) // (values.shape[dim] // shards_of)).reshape((-1,) + (1,) * (values.ndim - 1 - dim))

    first = jax.random.permutation(rng, shards_of)[block_of(target)]
    second = (block_of(target) + shards_of // 2) % shards_of
    return jnp.where((block_of(source) == first) | (block_of(source) == second), factor * values, values)


def steps_of(own_key, extent, pieces, low, largest):
    loudness, own = 1.0, jax.random.fold_in(own_key, 6)
    for dim, blocks in pieces:
        heights = jnp.exp(jax.random.uniform(jax.random.fold_in(own, dim), (blocks,), jnp.float32, low / len(pieces), largest / len(pieces)))
        loudness = loudness * jnp.repeat(heights, extent[dim] // blocks).reshape([-1 if axis == dim else 1 for axis in range(len(extent))])
    return loudness


def assign_block(stream_key, own, number, rows, number_of, top, reach, lean):
    sequence = jax.random.permutation(stream_key, number_of)
    crowded, common = shares(number_of, rows * top, reach, lean, True), shares(number_of, rows * top, reach, lean, False)
    places = jnp.arange(number_of)

    def named(lengths, turn):
        used = int((lengths > 0).sum())
        fixed = max(1, used // 4)
        shifted = fixed + (places - fixed + turn * (used - fixed)) % max(1, number_of - fixed)
        return jnp.zeros((number_of,), jnp.int32).at[sequence[jnp.where(places < fixed, places, shifted)]].set(jnp.asarray(lengths, jnp.int32))

    lengths = jnp.where(number % 4 == 0, named(crowded, number // 4), named(common, number - number // 4 - 1))
    mixed = jax.random.permutation(jax.random.fold_in(own, 3), number_of)
    source_of, taker = mixed[0:number_of // 2 * 2:2], mixed[1:number_of // 2 * 2:2]
    margin = jnp.minimum(lengths[source_of] - 1, reach - lengths[taker]) // 2
    margin = jnp.where((source_of == sequence[0]) | (taker == sequence[0]) | (lengths[taker] == 0), 0, jnp.maximum(margin, 0))
    shifted = jax.random.randint(jax.random.fold_in(own, 4), (number_of // 2,), 0, 1 << 20) % (margin + 1)
    lengths = lengths.at[source_of].add(-shifted).at[taker].add(shifted)
    labels = jnp.searchsorted(jnp.cumsum(lengths), jnp.arange(rows * top), side="right").astype(jnp.int32)
    grid = labels.reshape(top, rows).T
    grid = grid[jax.random.permutation(jax.random.fold_in(own, 1), rows)]
    turn = jax.random.randint(jax.random.fold_in(own, 2), (rows, 1), 0, top)
    return jnp.take_along_axis(grid, (jnp.arange(top)[None, :] + turn) % top, axis=1)


def shares(count, total, bound, lean, full):
    weights = [(1 << 20) // math.isqrt(standing ** lean) + 1 for standing in range(1, count + 1)]
    largest = bound if full else min(bound, max(-(-total // count), total * weights[0] // sum(weights)))
    least = 1 if total - largest >= count - 1 else 0
    given, rest = [largest] + [least] * (count - 1), total - largest - least * (count - 1)
    while rest > 0:
        candidates = [i for i in range(1, count) if given[i] < largest] or [i for i in range(1, count) if given[i] < bound]
        mass, left = sum([weights[i] for i in candidates]), rest
        for i in candidates:
            extra = min(bound - given[i], max(1, left * weights[i] // mass), rest)
            given[i] = given[i] + extra
            rest = rest - extra
    return np.array(given)


def noise(stream_key, shape, spread, bound, shards=(), kind=jnp.bfloat16):
    entries = jax.random.normal(stream_key, shape, jnp.float32) * spread
    if len(shards) > 0:
        entries = steps_of(stream_key, shape, shards, -0.22, 0.18) * entries
    return jnp.clip(entries, min=-bound, max=bound).astype(kind)


def gaussian_with(key, shape, spread, reach, split, heavy, held_as=jnp.bfloat16):
    entries = spread * jax.random.normal(key, shape, jnp.float32)
    if split:
        entries = entries * steps_of(key, shape, split, -0.22, 0.18)
    return jnp.clip(strengthened(entries, jax.random.fold_in(key, 3), *heavy), -reach, reach).astype(held_as)


def setup_inputs(seed: int = 0) -> dict:
    streams_of = jax.random.split(jax.random.key(seed), 9)
    tokens = gaussian_with(streams_of[0], (TOKENS, D), 1.0, 24.0, ((0, 256),), (0, 1, 256, 6.0))
    cotangent = gaussian_with(streams_of[1], (TOKENS, D), 1.0, 24.0, ((0, 256),), (0, 1, 256, 6.0))
    expert_ids_keys = jax.random.split(jax.random.fold_in(streams_of[2], 1), TOKENS // TOK_DEV)
    expert_ids_turns = jax.random.permutation(jax.random.fold_in(streams_of[2], 3), TOKENS // TOK_DEV)
    expert_ids = jax.vmap(lambda own, number: assign_block(jax.random.fold_in(streams_of[2], 2), own, number, TOK_DEV, EXPERTS, TOPK, CAP, 2))(expert_ids_keys, expert_ids_turns).reshape((TOKENS, TOPK))
    gate_weights = jnp.clip(jnp.exp(math.log(1.0) - 2.3025851 * jax.random.uniform(streams_of[3], (TOKENS, TOPK), jnp.float32) ** steps_of(streams_of[3], (TOKENS, TOPK), ((0, 256),), -0.2, 0.2)), 0.1, 1.0)
    partner = draw_partner(jax.random.fold_in(streams_of[8], 71), 0)
    w_gate = noise(streams_of[5], (EXPERTS, D, FF), D ** -0.5, 0.125, ((0, 8),))
    w_up = noise(streams_of[6], (EXPERTS, D, FF), D ** -0.5, 0.125, ((0, 8),))
    w_down = noise(streams_of[7], (EXPERTS, FF, D), FF ** -0.5, 0.21875, ((0, 8),))
    return dict(tokens=tokens, cotangent=cotangent, expert_ids=expert_ids, gate_weights=gate_weights, partner=partner, w_gate=w_gate, w_up=w_up, w_down=w_down)


def assign_slots(block_ids):
    flat_ids = block_ids.reshape(-1).astype(jnp.int32)
    one_hot = (flat_ids[:, None] == jnp.arange(EXPERTS, dtype=jnp.int32)[None, :]).astype(jnp.int32)
    earlier = (jnp.cumsum(one_hot, axis=0) - one_hot).astype(jnp.int32)
    position = jnp.sum(earlier * one_hot, axis=1).astype(jnp.int32)
    return (flat_ids * CAP + position).astype(jnp.int32)


def expert_pass(row_data, grads_in, gate_mat, up_mat, down_mat):
    gate_pre = jnp.dot(row_data, gate_mat, preferred_element_type=jnp.float32)
    up_pre = jnp.dot(row_data, up_mat, preferred_element_type=jnp.float32)
    sigmoid_gate = jax.nn.sigmoid(gate_pre)
    hidden = (gate_pre * sigmoid_gate * up_pre).astype(jnp.bfloat16)
    expert_out = jnp.dot(hidden, down_mat, preferred_element_type=jnp.float32).astype(jnp.bfloat16)
    hidden_grad = jnp.dot(grads_in, down_mat.T, preferred_element_type=jnp.float32)
    gate_grad_pre = (hidden_grad * up_pre * sigmoid_gate * (1.0 + gate_pre * (1.0 - sigmoid_gate))).astype(jnp.bfloat16)
    up_grad_pre = (hidden_grad * gate_pre * sigmoid_gate).astype(jnp.bfloat16)
    row_grad = (jnp.dot(gate_grad_pre, gate_mat.T, preferred_element_type=jnp.float32)
                + jnp.dot(up_grad_pre, up_mat.T, preferred_element_type=jnp.float32)).astype(jnp.bfloat16)
    part_gate = jnp.dot(row_data.T, gate_grad_pre, preferred_element_type=jnp.float32)
    part_up = jnp.dot(row_data.T, up_grad_pre, preferred_element_type=jnp.float32)
    part_down = jnp.dot(hidden.T, grads_in, preferred_element_type=jnp.float32)
    return expert_out, row_grad, part_gate, part_up, part_down


def take_rows(source_tab, index_tab):
    return jax.vmap(lambda one_tab, one_index: one_tab[one_index])(source_tab, index_tab)


def by_expert(buffered):
    return buffered.reshape(EXPERTS, EXPERTS, CAP, D).transpose(1, 0, 2, 3).reshape(EXPERTS, EXPERTS * CAP, D)


def reference(tokens, cotangent, expert_ids, gate_weights, partner, w_gate, w_up, w_down):
    per_row = EXPERTS * TOK_DEV
    assigns = TOK_DEV * TOPK

    def one_row(totals, row_input):
        row_tokens, row_cot, row_ids, row_gates = row_input
        slot_index = jax.vmap(assign_slots)(row_ids.reshape(EXPERTS, TOK_DEV, TOPK))
        repeated = jnp.repeat(row_tokens.reshape(EXPERTS, TOK_DEV, D), TOPK, axis=1)
        cot_float = row_cot.astype(jnp.float32)
        scaled = (row_gates[:, :, None] * cot_float[:, None, :]).astype(jnp.bfloat16).reshape(EXPERTS, assigns, D)
        filler = jnp.full((EXPERTS, EXPERTS * CAP), assigns, dtype=jnp.int32)
        source_ids = jnp.broadcast_to(jnp.arange(EXPERTS, dtype=jnp.int32)[:, None], (EXPERTS, assigns))
        assign_ids = jnp.broadcast_to(jnp.arange(assigns, dtype=jnp.int32)[None, :], (EXPERTS, assigns))
        lookup = filler.at[source_ids, slot_index].set(assign_ids)
        zero_row = jnp.zeros((EXPERTS, 1, D), jnp.bfloat16)
        buffer_x = take_rows(jnp.concatenate([repeated, zero_row], axis=1), lookup)
        buffer_g = take_rows(jnp.concatenate([scaled, zero_row], axis=1), lookup)
        results = lax.map(lambda item: expert_pass(*item),
                          (by_expert(buffer_x), by_expert(buffer_g), w_gate, w_up, w_down))
        expert_out, row_grad, part_gate, part_up, part_down = results
        per_assign = take_rows(by_expert(expert_out), slot_index).astype(jnp.float32).reshape(per_row, TOPK, D)
        mixed_out = jnp.sum(row_gates[:, :, None] * per_assign, axis=1).astype(jnp.bfloat16)
        gate_grad = jnp.sum(cot_float[:, None, :] * per_assign, axis=2)
        grad_rows = take_rows(by_expert(row_grad), slot_index).astype(jnp.float32).reshape(per_row, TOPK, D)
        token_grad = jnp.sum(grad_rows, axis=1).astype(jnp.bfloat16)
        new_totals = tuple(
            total_sum + lax.optimization_barrier(part_sum.astype(jnp.bfloat16)).astype(jnp.float32)
            for total_sum, part_sum in zip(totals, (part_gate, part_up, part_down)))
        return new_totals, (mixed_out, token_grad, gate_grad)

    inputs = (tokens.reshape(N_DP, per_row, D), cotangent.reshape(N_DP, per_row, D),
              expert_ids.reshape(N_DP, per_row, TOPK), gate_weights.reshape(N_DP, per_row, TOPK))
    start_sums = (jnp.zeros((EXPERTS, D, FF), jnp.float32), jnp.zeros((EXPERTS, D, FF), jnp.float32),
                  jnp.zeros((EXPERTS, FF, D), jnp.float32))
    sums_all, outputs = lax.scan(one_row, start_sums, inputs)
    mixed_out, token_grad, gate_grad = outputs
    slot_grad_gate = jnp.take(sums_all[0], partner, axis=0)
    slot_grad_up = jnp.take(sums_all[1], partner, axis=0)
    slot_grad_down = jnp.take(sums_all[2], partner, axis=0)
    return (mixed_out.reshape(TOKENS, D), token_grad.reshape(TOKENS, D), gate_grad.reshape(TOKENS, TOPK),
            slot_grad_gate, slot_grad_up, slot_grad_down)
```

```python
import jax
import jax.numpy as jnp
from jax import lax
from jax.sharding import PartitionSpec as P


def contract_rows(left_mat, right_mat):
    return lax.dot_general(
        left_mat, right_mat, (((0,), (0,)), ((), ())), preferred_element_type=jnp.float32
    )


def contract_cols(left_mat, right_mat):
    return lax.dot_general(
        left_mat, right_mat, (((1,), (1,)), ((), ())), preferred_element_type=jnp.float32
    )


def pick_from(stacked, source):
    return lax.dynamic_index_in_dim(stacked, source, 0, keepdims=False)


def shards(tokens, cotangent, expert_ids, gate_weights, partner, w_gate, w_up, w_down):
    groups = lax.axis_size("expert")
    my_group = lax.axis_index("expert")
    tok_count, model_width = tokens.shape
    top_count = expert_ids.shape[1]
    capacity = min(tok_count, 5 * tok_count * top_count // (4 * groups))
    buffer_rows = groups * capacity
    group_ids = jnp.arange(groups, dtype=jnp.int32)
    my_mate = pick_from(partner, my_group)
    flat_ids = expert_ids.reshape(-1)
    dest_group = flat_ids
    one_hot = (dest_group[:, None] == group_ids[None, :]).astype(jnp.int32)
    earlier = jnp.cumsum(one_hot, axis=0) - one_hot
    slot_index = dest_group * capacity + jnp.sum(earlier * one_hot, axis=1)
    place_mat = (slot_index[None, :] == jnp.arange(buffer_rows, dtype=jnp.int32)[:, None]).astype(
        jnp.bfloat16
    )
    gate_mat, up_mat, down_mat = w_gate[0], w_up[0], w_down[0]
    repeated = jnp.repeat(tokens, top_count, axis=0)
    outgoing_rows = jnp.dot(place_mat, repeated, preferred_element_type=jnp.float32).astype(
        jnp.bfloat16
    )
    expert_in = lax.all_to_all(
        outgoing_rows.reshape(groups, capacity, model_width),
        "expert",
        split_axis=0,
        concat_axis=0,
        tiled=True,
    ).reshape(buffer_rows, model_width)
    gate_pre = jnp.dot(expert_in, gate_mat, preferred_element_type=jnp.float32)
    up_pre = jnp.dot(expert_in, up_mat, preferred_element_type=jnp.float32)
    sigmoid_gate = jax.nn.sigmoid(gate_pre)
    hidden = (gate_pre * sigmoid_gate * up_pre).astype(jnp.bfloat16)
    expert_out = jnp.dot(hidden, down_mat, preferred_element_type=jnp.float32).astype(jnp.bfloat16)
    returned = lax.all_to_all(
        expert_out.reshape(groups, capacity, model_width),
        "expert",
        split_axis=0,
        concat_axis=0,
        tiled=True,
    ).reshape(buffer_rows, model_width)
    per_assign = (
        jnp.take(returned, slot_index, axis=0)
        .astype(jnp.float32)
        .reshape(tok_count, top_count, model_width)
    )
    mixed_out = jnp.sum(gate_weights[:, :, None] * per_assign, axis=1).astype(jnp.bfloat16)
    cot_float = cotangent.astype(jnp.float32)
    gate_grad = jnp.sum(cot_float[:, None, :] * per_assign, axis=2)
    scaled = (
        (gate_weights[:, :, None] * cot_float[:, None, :])
        .astype(jnp.bfloat16)
        .reshape(-1, model_width)
    )
    outgoing_grads = jnp.dot(place_mat, scaled, preferred_element_type=jnp.float32).astype(
        jnp.bfloat16
    )
    grads_in = lax.all_to_all(
        outgoing_grads.reshape(groups, capacity, model_width),
        "expert",
        split_axis=0,
        concat_axis=0,
        tiled=True,
    ).reshape(buffer_rows, model_width)
    hidden_grad = contract_cols(grads_in, down_mat)
    gate_grad_pre = (
        hidden_grad * up_pre * sigmoid_gate * (1.0 + gate_pre * (1.0 - sigmoid_gate))
    ).astype(jnp.bfloat16)
    up_grad_pre = (hidden_grad * gate_pre * sigmoid_gate).astype(jnp.bfloat16)
    row_grad = (contract_cols(gate_grad_pre, gate_mat) + contract_cols(up_grad_pre, up_mat)).astype(
        jnp.bfloat16
    )
    returned_grads = lax.all_to_all(
        row_grad.reshape(groups, capacity, model_width),
        "expert",
        split_axis=0,
        concat_axis=0,
        tiled=True,
    ).reshape(buffer_rows, model_width)
    grad_rows = (
        jnp.take(returned_grads, slot_index, axis=0)
        .astype(jnp.float32)
        .reshape(tok_count, top_count, model_width)
    )
    token_grad = jnp.sum(grad_rows, axis=1).astype(jnp.bfloat16)
    partial_gate = contract_rows(expert_in, gate_grad_pre)
    partial_up = contract_rows(expert_in, up_grad_pre)
    partial_down = contract_rows(hidden, grads_in)
    share_gate = lax.psum_scatter(
        partial_gate.astype(jnp.bfloat16), "dp", scatter_dimension=0, tiled=True
    )
    share_up = lax.psum_scatter(
        partial_up.astype(jnp.bfloat16), "dp", scatter_dimension=0, tiled=True
    )
    share_down = lax.psum_scatter(
        partial_down.astype(jnp.bfloat16), "dp", scatter_dimension=1, tiled=True
    )
    sums = tuple(
        pick_from(lax.all_gather(share, "expert", axis=0), my_mate).astype(jnp.float32)
        for share in (share_gate, share_up, share_down)
    )
    return (mixed_out, token_grad, gate_grad, sums[0][None], sums[1][None], sums[2][None])


def solution(mesh):
    in_specs = (
        P(("dp", "expert"), None),
        P(("dp", "expert"), None),
        P(("dp", "expert"), None),
        P(("dp", "expert"), None),
        P(),
        P("expert", None, None),
        P("expert", None, None),
        P("expert", None, None),
    )
    out_specs = (
        P(("dp", "expert"), None),
        P(("dp", "expert"), None),
        P(("dp", "expert"), None),
        P("expert", "dp", None),
        P("expert", "dp", None),
        P("expert", None, "dp"),
    )
    return jax.shard_map(shards, mesh=mesh, in_specs=in_specs, out_specs=out_specs, check_vma=False)
```

```python
import functools

import jax
import jax.numpy as jnp
from jax import lax
from jax.experimental import pallas as pl
from jax.experimental.pallas import tpu as pltpu
from jax.sharding import PartitionSpec as P

MESH = pl.DeviceIdType.MESH
RING = 8
STEPS = RING - 1
ORDER_UP = (0, 2, 4, 6, 5, 3, 1, 7)
ORDER_DOWN = (1, 3, 5, 6, 4, 2, 0, 7)


def remote(src, dst, send_sem, recv_sem, dp, ex):
    return pltpu.make_async_remote_copy(
        src_ref=src,
        dst_ref=dst,
        send_sem=send_sem,
        recv_sem=recv_sem,
        device_id=(dp, ex),
        device_id_type=MESH,
    )


def reduce_kernel(
    partner_ref, x_ref, g_ref, gate_ref, up_ref, hid_ref,
    out_gate, out_up, out_down,
    part, pair_in, ring_out, ring_in, kept, cross_out, cross_in, share, gathered,
    pair_s, pair_r, ring_s, ring_r, cross_s, cross_r, ex_s, ex_r,
):
    dp = lax.axis_index("dp")
    ex = lax.axis_index("expert")
    z, half, core = dp // 4, (dp // 2) % 2, dp % 2
    ex_x, ex_y = ex // 2, ex % 2

    def at(zz, hh, cc):
        return zz * 4 + hh * 2 + cc

    mate = at(z, half, 1 - core)
    after = at((z + 1) % RING, half, core)
    before = at((z + RING - 1) % RING, half, core)
    across = at(z, 1 - half, core)
    offsets = [(dx, dy) for dx in range(4) for dy in range(2) if (dx, dy) != (0, 0)]

    def peer(dx, dy):
        return ((ex_x + dx) % 4) * 2 + (ex_y + dy) % 2

    def source(dx, dy):
        return ((ex_x + 4 - dx) % 4) * 2 + (ex_y + 2 - dy) % 2

    barrier = pltpu.get_barrier_semaphore()
    for other in (mate, after, before, across):
        pl.semaphore_signal(barrier, inc=1, device_id=(other, ex), device_id_type=MESH)
    for dx, dy in offsets:
        pl.semaphore_signal(barrier, inc=1, device_id=(dp, peer(dx, dy)), device_id_type=MESH)
    pl.semaphore_wait(barrier, 4 + len(offsets))

    lefts = (x_ref, x_ref, g_ref)
    rights = (gate_ref, up_ref, hid_ref)
    outs = (out_gate, out_up, out_down)

    def chunk_of(k):
        shift = (RING - 1 - k // 2) if k % 2 == 0 else (k // 2 + 1) % 4
        return (z + shift) % RING

    def pair_copy(k, m):
        return remote(
            part.at[k, m, 1 - core], pair_in.at[k, m],
            pair_s.at[k, m], pair_r.at[k, m], mate, ex,
        )

    def produce(k):
        start = pl.multiple_of(chunk_of(k) * 256, 256)
        for m in range(3):
            block = lax.dot_general(
                lefts[m][:, pl.ds(start, 256)], rights[m][...],
                (((0,), (0,)), ((), ())), preferred_element_type=jnp.float32,
            ).astype(jnp.bfloat16)
            for hh in range(2):
                for cc in range(2):
                    row = (hh * 2 + cc) * 64
                    part[k, m, cc, hh] = block[row:row + 64]
            pair_copy(k, m).start()

    paired = set()

    def local_sum(k, m, way):
        if (k, m) not in paired:
            paired.add((k, m))
            pair_copy(k, m).wait()
        return part[k, m, core, way].astype(jnp.float32) + pair_in[k, m, way].astype(jnp.float32)

    def ring_copy(m, way, s):
        return remote(
            ring_out.at[m, way, s], ring_in.at[m, way, s],
            ring_s.at[m, way, s], ring_r.at[m, way, s],
            after if way == 0 else before, ex,
        )

    def ring(s, m):
        for way, order in enumerate((ORDER_UP, ORDER_DOWN)):
            value = local_sum(order[s], m, way)
            if s > 0:
                ring_copy(m, way, s - 1).wait()
                value = value + ring_in[m, way, s - 1].astype(jnp.float32)
            if s < STEPS:
                ring_out[m, way, s] = value.astype(jnp.bfloat16)
                ring_copy(m, way, s).start()
            else:
                kept[m, way] = value
                cross_out[m, way] = value.astype(jnp.bfloat16)

    def cross_copy(m):
        return remote(
            cross_out.at[m, 1 - half], cross_in.at[m],
            cross_s.at[m], cross_r.at[m], across, ex,
        )

    def share_copy(m, i):
        dx, dy = offsets[i]
        return remote(
            share.at[m], gathered.at[m, ex],
            ex_s.at[m, i], ex_r.at[m, i], dp, peer(dx, dy),
        )

    produce(0)
    produce(1)
    for s in range(STEPS + 1):
        if s < 3:
            produce(2 * s + 2)
            produce(2 * s + 3)
        for m in range(3):
            ring(s, m)
            if s == STEPS:
                cross_copy(m).start()
    for m in range(3):
        cross_copy(m).wait()
        total = (kept[m, half] + cross_in[m].astype(jnp.float32)).astype(jnp.bfloat16)
        share[m] = total
        gathered[m, ex] = total
        for i in range(len(offsets)):
            share_copy(m, i).start()
    mine = partner_ref[ex]
    for m in range(3):
        for i in range(len(offsets)):
            share_copy(m, i).wait()
    for m in range(3):
        outs[m][...] = gathered[m, mine].astype(jnp.float32)


def reduce_grads(partner, x, g, gate, up, hid):
    bf, f32 = jnp.bfloat16, jnp.float32
    vmem = pl.BlockSpec(memory_space=pltpu.VMEM)
    dma = pltpu.SemaphoreType.DMA
    width = gate.shape[1]
    return pl.pallas_call(
        reduce_kernel,
        out_shape=[jax.ShapeDtypeStruct((64, width), f32)] * 3,
        in_specs=[pl.BlockSpec(memory_space=pltpu.SMEM)] + [vmem] * 5,
        out_specs=[vmem] * 3,
        scratch_shapes=[
            pltpu.VMEM((RING, 3, 2, 2, 64, width), bf),
            pltpu.VMEM((RING, 3, 2, 64, width), bf),
            pltpu.VMEM((3, 2, STEPS, 64, width), bf),
            pltpu.VMEM((3, 2, STEPS, 64, width), bf),
            pltpu.VMEM((3, 2, 64, width), f32),
            pltpu.VMEM((3, 2, 64, width), bf),
            pltpu.VMEM((3, 64, width), bf),
            pltpu.VMEM((3, 64, width), bf),
            pltpu.VMEM((3, 8, 64, width), bf),
            dma((RING, 3)), dma((RING, 3)),
            dma((3, 2, STEPS)), dma((3, 2, STEPS)),
            dma((3,)), dma((3,)),
            dma((3, 7)), dma((3, 7)),
        ],
        compiler_params=pltpu.CompilerParams(
            collective_id=0, has_side_effects=True, vmem_limit_bytes=60 * 1024 * 1024
        ),
    )(partner, x, g, gate, up, hid)


def contract_cols(left_mat, right_mat):
    return lax.dot_general(
        left_mat, right_mat, (((1,), (1,)), ((), ())), preferred_element_type=jnp.float32
    )


def shards(tokens, cotangent, expert_ids, gate_weights, partner, w_gate, w_up, w_down):
    groups = lax.axis_size("expert")
    my_group = lax.axis_index("expert")
    tok_count, model_width = tokens.shape
    top_count = expert_ids.shape[1]
    capacity = min(tok_count, 5 * tok_count * top_count // (4 * groups))
    buffer_rows = groups * capacity
    group_ids = jnp.arange(groups, dtype=jnp.int32)
    flat_ids = expert_ids.reshape(-1)
    dest_group = flat_ids
    one_hot = (dest_group[:, None] == group_ids[None, :]).astype(jnp.int32)
    earlier = jnp.cumsum(one_hot, axis=0) - one_hot
    slot_index = dest_group * capacity + jnp.sum(earlier * one_hot, axis=1)
    place_mat = (slot_index[None, :] == jnp.arange(buffer_rows, dtype=jnp.int32)[:, None]).astype(
        jnp.bfloat16
    )
    gate_mat, up_mat, down_mat = w_gate[0], w_up[0], w_down[0]
    repeated = jnp.repeat(tokens, top_count, axis=0)
    outgoing_rows = jnp.dot(place_mat, repeated, preferred_element_type=jnp.float32).astype(
        jnp.bfloat16
    )
    expert_in = lax.all_to_all(
        outgoing_rows.reshape(groups, capacity, model_width),
        "expert",
        split_axis=0,
        concat_axis=0,
        tiled=True,
    ).reshape(buffer_rows, model_width)
    gate_pre = jnp.dot(expert_in, gate_mat, preferred_element_type=jnp.float32)
    up_pre = jnp.dot(expert_in, up_mat, preferred_element_type=jnp.float32)
    sigmoid_gate = jax.nn.sigmoid(gate_pre)
    hidden = (gate_pre * sigmoid_gate * up_pre).astype(jnp.bfloat16)
    expert_out = jnp.dot(hidden, down_mat, preferred_element_type=jnp.float32).astype(jnp.bfloat16)
    returned = lax.all_to_all(
        expert_out.reshape(groups, capacity, model_width),
        "expert",
        split_axis=0,
        concat_axis=0,
        tiled=True,
    ).reshape(buffer_rows, model_width)
    per_assign = (
        jnp.take(returned, slot_index, axis=0)
        .astype(jnp.float32)
        .reshape(tok_count, top_count, model_width)
    )
    mixed_out = jnp.sum(gate_weights[:, :, None] * per_assign, axis=1).astype(jnp.bfloat16)
    cot_float = cotangent.astype(jnp.float32)
    gate_grad = jnp.sum(cot_float[:, None, :] * per_assign, axis=2)
    scaled = (
        (gate_weights[:, :, None] * cot_float[:, None, :])
        .astype(jnp.bfloat16)
        .reshape(-1, model_width)
    )
    outgoing_grads = jnp.dot(place_mat, scaled, preferred_element_type=jnp.float32).astype(
        jnp.bfloat16
    )
    grads_in = lax.all_to_all(
        outgoing_grads.reshape(groups, capacity, model_width),
        "expert",
        split_axis=0,
        concat_axis=0,
        tiled=True,
    ).reshape(buffer_rows, model_width)
    hidden_grad = contract_cols(grads_in, down_mat)
    gate_grad_pre = (
        hidden_grad * up_pre * sigmoid_gate * (1.0 + gate_pre * (1.0 - sigmoid_gate))
    ).astype(jnp.bfloat16)
    up_grad_pre = (hidden_grad * gate_pre * sigmoid_gate).astype(jnp.bfloat16)
    row_grad = (contract_cols(gate_grad_pre, gate_mat) + contract_cols(up_grad_pre, up_mat)).astype(
        jnp.bfloat16
    )
    returned_grads = lax.all_to_all(
        row_grad.reshape(groups, capacity, model_width),
        "expert",
        split_axis=0,
        concat_axis=0,
        tiled=True,
    ).reshape(buffer_rows, model_width)
    grad_rows = (
        jnp.take(returned_grads, slot_index, axis=0)
        .astype(jnp.float32)
        .reshape(tok_count, top_count, model_width)
    )
    token_grad = jnp.sum(grad_rows, axis=1).astype(jnp.bfloat16)
    sum_gate, sum_up, sum_down = reduce_grads(
        partner, expert_in, grads_in, gate_grad_pre, up_grad_pre, hidden
    )
    return (mixed_out, token_grad, gate_grad, sum_gate[None], sum_up[None], sum_down.T[None])


def solution(mesh):
    in_specs = (
        P(("dp", "expert"), None),
        P(("dp", "expert"), None),
        P(("dp", "expert"), None),
        P(("dp", "expert"), None),
        P(),
        P("expert", None, None),
        P("expert", None, None),
        P("expert", None, None),
    )
    out_specs = (
        P(("dp", "expert"), None),
        P(("dp", "expert"), None),
        P(("dp", "expert"), None),
        P("expert", "dp", None),
        P("expert", "dp", None),
        P("expert", None, "dp"),
    )
    return jax.shard_map(shards, mesh=mesh, in_specs=in_specs, out_specs=out_specs, check_vma=False)
```

```python
import jax
import jax.numpy as jnp
from jax import lax
from jax.experimental import pallas as pl
from jax.experimental.pallas import tpu as pltpu
from jax.sharding import PartitionSpec as P

MESH = pl.DeviceIdType.MESH
BF, F32 = jnp.bfloat16, jnp.float32
RING = 8
STEPS = RING - 1
GROUPS = 4
ORDER_UP = (0, 2, 4, 6, 5, 3, 1, 7)
ORDER_DOWN = (1, 3, 5, 6, 4, 2, 0, 7)
ACROSS_X = (1, 3, 2)
DOWN, GATE, UP = 0, 1, 2
PIECES = 6


def remote(src, dst, send_sem, recv_sem, dp, ex):
    return pltpu.make_async_remote_copy(
        src_ref=src,
        dst_ref=dst,
        send_sem=send_sem,
        recv_sem=recv_sem,
        device_id=(dp, ex),
        device_id_type=MESH,
    )


def rows_by_rows(left, right):
    return lax.dot_general(left, right, (((0,), (0,)), ((), ())), preferred_element_type=F32)


def cols_by_cols(left, right):
    return lax.dot_general(left, right, (((1,), (1,)), ((), ())), preferred_element_type=F32)


def plain(left, right):
    return jnp.dot(left, right, preferred_element_type=F32)


def step_kernel(
    partner_ref, tok_ref, cot_ref, ids_ref, gw_ref, wg_hbm, wu_hbm, wd_hbm,
    mixed_ref, token_ref, ggrad_ref, shares_ref,
    wg, wu, wd, cols_ref, sel_t, pick_ref, mix_ref, any_ref,
    tok_y, cot_y, ids_y, gw_y,
    x_out, x_in, g_out, g_in, e_out, e_in, r_out, r_in,
    m_out, m_in, t_out, t_in, gg_out, gg_in,
    gate_pre, up_pre, hid_grad, hid, ggp, ugp, scores,
    part, pair_in, ring_out, ring_in, kept, cross_out, cross_in, share,
    row_0, row_1, row_2, row_3, row_4, row_5, chosen, other_row,
    w_sem, own_sem, act_s, act_r, y_s, y_r, small_s, small_r,
    pair_s, pair_r, ring_s, ring_r, cross_s, cross_r, ex_s, ex_r, last_s, last_r,
):
    in_row = (row_0, row_1, row_2, row_3, row_4, row_5)
    dp = lax.axis_index("dp")
    ex = lax.axis_index("expert")
    z, half, core = dp // 4, (dp // 2) % 2, dp % 2
    ex_x, ex_y = ex // 2, ex % 2
    tok_count = tok_ref.shape[0]
    slots = x_in.shape[1]
    block = slots // 4
    cap = block // 2
    width = x_in.shape[2]
    share_rows = share.shape[1]
    piece_width = share.shape[2]

    def at(zz, hh, cc):
        return zz * 4 + hh * 2 + cc

    mate = at(z, half, 1 - core)
    after = at((z + 1) % RING, half, core)
    before = at((z + RING - 1) % RING, half, core)
    across = at(z, 1 - half, core)
    twin = ex_x * 2 + 1 - ex_y

    def peer(dx):
        return ((ex_x + dx) % 4) * 2 + ex_y

    def chunk_of(k):
        shift = (RING - 1 - k // 2) if k % 2 == 0 else (k // 2 + 1) % 4
        return (z + shift) % RING

    def columns(k):
        return pl.ds(pl.multiple_of(chunk_of(k) * width, width), width)

    def weight_copies(s):
        copies = []
        for k in (2 * s, 2 * s + 1):
            copies.append(pltpu.make_async_copy(wg_hbm.at[columns(k)], wg.at[k], w_sem.at[0, k]))
            copies.append(pltpu.make_async_copy(wu_hbm.at[columns(k)], wu.at[k], w_sem.at[1, k]))
        return copies

    def down_copies(s):
        return [
            pltpu.make_async_copy(wd_hbm.at[:, columns(k)], wd.at[k], w_sem.at[2, k])
            for k in (2 * s, 2 * s + 1)
        ]

    barrier = pltpu.get_barrier_semaphore()
    for other in (mate, after, before, across):
        pl.semaphore_signal(barrier, inc=1, device_id=(other, ex), device_id_type=MESH)
    for other in [twin] + [peer(dx) for dx in ACROSS_X]:
        pl.semaphore_signal(barrier, inc=1, device_id=(dp, other), device_id_type=MESH)
    for s in range(GROUPS):
        for copy in weight_copies(s):
            copy.start()
    for s in range(GROUPS):
        for copy in down_copies(s):
            copy.start()

    def y_copy(kind, k):
        src, dst = (
            (tok_ref.at[:, columns(k)], tok_y.at[k]),
            (cot_ref.at[:, columns(k)], cot_y.at[k]),
            (m_out.at[k], m_in.at[k]),
            (t_out.at[k], t_in.at[k]),
        )[kind]
        return remote(src, dst, y_s.at[kind, k], y_r.at[kind, k], dp, twin)

    def small_copy(i):
        src, dst = ((ids_ref, ids_y), (gw_ref, gw_y), (gg_out, gg_in))[i]
        return remote(src, dst, small_s.at[i], small_r.at[i], dp, twin)

    lanes = lax.broadcasted_iota(jnp.int32, (tok_count, tok_count), 1)
    rows = lax.broadcasted_iota(jnp.int32, (tok_count, tok_count), 0)
    zero = jnp.zeros((tok_count, tok_count), F32)
    below = jnp.where(lanes < rows, 1.0, zero).astype(BF)
    lane_of = lanes.astype(F32)
    this_row = lanes % 2 == ex_y
    pad = 384
    wide = lax.broadcasted_iota(jnp.int32, (tok_count, pad), 1).astype(F32)
    wide_zero = jnp.zeros((tok_count, pad), F32)
    top = ids_ref.shape[0]

    def route(q, ids, weights):
        cols_ref[q] = zero
        cols_ref[q, 0:top] = ids[...].astype(F32)
        cols_ref[q, top:2 * top] = weights[...]
        cols_ref[q] = jnp.transpose(cols_ref[q])
        hits = [cols_ref[q, :, i:i + 1] == lane_of for i in range(top)]
        named = jnp.where(hits[0] | hits[1], 1.0, zero).astype(BF)
        place = plain(below, named) + (lanes // 2).astype(F32) * float(block)
        place = place + float(q * cap + 1)
        picks = []
        for hit in hits:
            slot = jnp.sum(jnp.where(hit & this_row, place, zero), axis=1, keepdims=True) - 1.0
            picks.append(jnp.where(slot == wide, 1.0, wide_zero))
        both = jnp.concatenate(picks, axis=0)
        pick_ref[2 * q * tok_count:2 * (q + 1) * tok_count] = both[:, :slots]
        sel_t[:, 2 * q * tok_count:2 * (q + 1) * tok_count] = jnp.transpose(both)[:slots].astype(BF)
        any_ref[q * tok_count:(q + 1) * tok_count] = (picks[0] + picks[1])[:, :slots].astype(BF)
        mix = picks[0] * cols_ref[q, :, top:top + 1] + picks[1] * cols_ref[q, :, top + 1:top + 2]
        mix = mix[:, :slots]
        coarse = mix.astype(BF)
        mix_ref[2 * q * tok_count:(2 * q + 1) * tok_count] = coarse
        mix_ref[(2 * q + 1) * tok_count:(2 * q + 2) * tok_count] = (mix - coarse.astype(F32)).astype(BF)

    route(0, ids_ref, gw_ref)
    pl.semaphore_wait(barrier, 8)
    for i in range(2):
        small_copy(i).start()
    for kind in range(2):
        for k in range(RING):
            y_copy(kind, k).start()
    for i in range(2):
        small_copy(i).wait()
    route(1, ids_y, gw_y)

    def block_rows(owner):
        return pl.ds(pl.multiple_of(owner * block, 8), block)

    def act_copies(kind, src, dst, s):
        pairs = pl.ds(2 * s, 2)
        copies = []
        for i, dx in enumerate(ACROSS_X):
            copies.append(remote(
                src.at[pairs, block_rows((ex_x + dx) % 4)], dst.at[pairs, block_rows(ex_x)],
                act_s.at[kind, s, i], act_r.at[kind, s, i], dp, peer(dx),
            ))
        copies.append(pltpu.make_async_copy(
            src.at[pairs, block_rows(ex_x)], dst.at[pairs, block_rows(ex_x)], own_sem.at[kind, s]
        ))
        return copies

    def send(kind, src, dst, s):
        for copy in act_copies(kind, src, dst, s):
            copy.start()

    def arrive(kind, src, dst, s):
        for copy in act_copies(kind, src, dst, s):
            copy.wait()

    sel_any = jnp.concatenate(
        [
            sel_t[:, 0:tok_count] + sel_t[:, tok_count:2 * tok_count],
            sel_t[:, 2 * tok_count:3 * tok_count] + sel_t[:, 3 * tok_count:],
        ],
        axis=1,
    )
    for s in range(GROUPS):
        for k in (2 * s, 2 * s + 1):
            y_copy(0, k).wait()
            both = jnp.concatenate([tok_ref[:, columns(k)], tok_y[k]], axis=0)
            x_out[k] = plain(sel_any, both).astype(BF)
        send(0, x_out, x_in, s)

    def scaled_rows(q, values):
        values = values.astype(F32)
        return [(cols_ref[q, :, top + i:top + i + 1] * values).astype(BF) for i in range(top)]

    def dispatch_grads(s):
        for k in (2 * s, 2 * s + 1):
            y_copy(1, k).wait()
            scaled = scaled_rows(0, cot_ref[:, columns(k)]) + scaled_rows(1, cot_y[k])
            g_out[k] = plain(sel_t[...], jnp.concatenate(scaled, axis=0)).astype(BF)
        send(1, g_out, g_in, s)

    def pair_copy(p, k):
        return remote(
            part.at[p, k, 1 - core], pair_in.at[p, k],
            pair_s.at[p, k], pair_r.at[p, k], mate, ex,
        )

    def produce(m, k):
        left = g_in if m == DOWN else x_in
        right = (hid, ggp, ugp)[m]
        grad = rows_by_rows(left[k], right[...]).astype(BF)
        for p in (2 * m, 2 * m + 1):
            col = (p % 2) * piece_width
            for hh in range(2):
                for cc in range(2):
                    row = (hh * 2 + cc) * share_rows
                    part[p, k, cc, hh] = grad[row:row + share_rows, col:col + piece_width]
            pair_copy(p, k).start()

    paired = set()

    def local_sum(p, k, way):
        if (p, k) not in paired:
            paired.add((p, k))
            pair_copy(p, k).wait()
        return part[p, k, core, way].astype(F32) + pair_in[p, k, way].astype(F32)

    def ring_copy(p, way, s):
        return remote(
            ring_out.at[p, way, s], ring_in.at[p, way, s],
            ring_s.at[p, way, s], ring_r.at[p, way, s],
            after if way == 0 else before, ex,
        )

    def cross_copy(p):
        return remote(
            cross_out.at[p, 1 - half], cross_in.at[p],
            cross_s.at[p], cross_r.at[p], across, ex,
        )

    def ring_piece(p, s):
        for way, order in enumerate((ORDER_UP, ORDER_DOWN)):
            value = local_sum(p, order[s], way)
            if s > 0:
                ring_copy(p, way, s - 1).wait()
                value = value + ring_in[p, way, s - 1].astype(F32)
            if s < STEPS:
                ring_out[p, way, s] = value.astype(BF)
                ring_copy(p, way, s).start()
            else:
                kept[p, way] = value
                cross_out[p, way] = value.astype(BF)
        if s == STEPS:
            cross_copy(p).start()

    def ring(m, s):
        ring_piece(2 * m, s)
        ring_piece(2 * m + 1, s)

    def share_copy(p, i):
        return remote(
            share.at[p], in_row[p].at[ex_x],
            ex_s.at[p, i], ex_r.at[p, i], dp, peer(ACROSS_X[i]),
        )

    def last_copy(p):
        return remote(chosen.at[p], other_row.at[p], last_s.at[p], last_r.at[p], dp, twin)

    def spread(p):
        cross_copy(p).wait()
        total = (kept[p, half] + cross_in[p].astype(F32)).astype(BF)
        share[p] = total
        in_row[p][ex_x] = total
        for i in range(3):
            share_copy(p, i).start()

    def hand_over(p):
        for i in range(3):
            share_copy(p, i).wait()
        chosen[p] = in_row[p][partner_ref[twin] // 2]
        last_copy(p).start()

    def conclude(p):
        last_copy(p).wait()
        mine = partner_ref[ex]
        near = jnp.full((share_rows, piece_width), mine % 2, jnp.int32) == ex_y
        col = (p % 2) * piece_width
        value = jnp.where(near, in_row[p][mine // 2].astype(F32), other_row[p].astype(F32))
        shares_ref[p // 2, :, col:col + piece_width] = value.astype(BF)

    for s in range(GROUPS):
        dispatch_grads(s)
        arrive(0, x_out, x_in, s)
        for copy in weight_copies(s):
            copy.wait()
        lo, hi = 2 * s, 2 * s + 1
        gate_term = plain(x_in[lo], wg[lo]) + plain(x_in[hi], wg[hi])
        gate_pre[...] = gate_term if s == 0 else gate_pre[...] + gate_term
        up_term = plain(x_in[lo], wu[lo]) + plain(x_in[hi], wu[hi])
        up_pre[...] = up_term if s == 0 else up_pre[...] + up_term
    gate_value = gate_pre[...]
    hid[...] = (gate_value * jax.nn.sigmoid(gate_value) * up_pre[...]).astype(BF)

    def expert_out(s):
        for k in (2 * s, 2 * s + 1):
            e_out[k] = plain(hid[...], wd[k]).astype(BF)
        send(2, e_out, e_in, s)

    def row_grad(s):
        for k in (2 * s, 2 * s + 1):
            r_out[k] = (cols_by_cols(ggp[...], wg[k]) + cols_by_cols(ugp[...], wu[k])).astype(BF)
        send(3, r_out, r_in, s)

    def mixed_theirs(s):
        arrive(2, e_out, e_in, s)
        for k in (2 * s, 2 * s + 1):
            both_parts = plain(mix_ref[2 * tok_count:], e_in[k])
            m_out[k] = (both_parts[:tok_count] + both_parts[tok_count:]).astype(BF)
            y_copy(2, k).start()
            cots = jnp.concatenate([cot_ref[:, columns(k)], cot_y[k]], axis=0)
            score = cols_by_cols(cots, e_in[k])
            scores[...] = score if k == 0 else scores[...] + score

    def mixed_mine(s):
        for k in (2 * s, 2 * s + 1):
            y_copy(2, k).wait()
            both_parts = plain(mix_ref[:2 * tok_count], e_in[k])
            total = both_parts[:tok_count] + both_parts[tok_count:] + m_in[k].astype(F32)
            mixed_ref[:, columns(k)] = total.astype(BF)

    def gate_grad(q):
        found = []
        for i in range(top):
            row = (2 * q + i) * tok_count
            product = pick_ref[row:row + tok_count] * scores[q * tok_count:(q + 1) * tok_count]
            found.append(jnp.sum(product, axis=1, keepdims=True))
        spot = jnp.where(lanes == 0, found[0], zero) + jnp.where(lanes == 1, found[1], zero)
        return jnp.transpose(spot)[:8]

    def gate_grad_theirs():
        gg_out[...] = gate_grad(1)
        small_copy(2).start()

    def gate_grad_mine():
        small_copy(2).wait()
        ggrad_ref[...] = gate_grad(0) + gg_in[...]

    def token_theirs(s):
        arrive(3, r_out, r_in, s)
        for k in (2 * s, 2 * s + 1):
            t_out[k] = plain(any_ref[tok_count:], r_in[k]).astype(BF)
            y_copy(3, k).start()

    def token_mine(s):
        for k in (2 * s, 2 * s + 1):
            y_copy(3, k).wait()
            total = plain(any_ref[:tok_count], r_in[k]) + t_in[k].astype(F32)
            token_ref[:, columns(k)] = total.astype(BF)

    for s in range(GROUPS):
        for copy in down_copies(s):
            copy.wait()
    for s in range(GROUPS):
        arrive(1, g_out, g_in, s)
        lo, hi = 2 * s, 2 * s + 1
        produce(DOWN, lo)
        produce(DOWN, hi)
        term = cols_by_cols(g_in[lo], wd[lo]) + cols_by_cols(g_in[hi], wd[hi])
        hid_grad[...] = term if s == 0 else hid_grad[...] + term
        if s < 3:
            ring(DOWN, s)
        expert_out(s)

    gate_value = gate_pre[...]
    sig = jax.nn.sigmoid(gate_value)
    grad = hid_grad[...] * sig
    ggp[...] = (grad * up_pre[...] * (1.0 + gate_value * (1.0 - sig))).astype(BF)
    ugp[...] = (grad * gate_value).astype(BF)

    produce(GATE, 0)
    produce(GATE, 1)
    ring(DOWN, 3)
    produce(UP, 0)
    produce(UP, 1)
    ring(GATE, 0)
    row_grad(0)
    ring(DOWN, 4)
    ring(UP, 0)
    for k in (2, 3):
        produce(GATE, k)
        produce(UP, k)
    ring(GATE, 1)
    row_grad(1)
    ring(DOWN, 5)
    ring(UP, 1)
    for k in (4, 5):
        produce(GATE, k)
        produce(UP, k)
    ring(GATE, 2)
    row_grad(2)
    mixed_theirs(0)
    ring(DOWN, 6)
    ring(UP, 2)
    for k in (6, 7):
        produce(GATE, k)
        produce(UP, k)
    ring(GATE, 3)
    row_grad(3)
    mixed_theirs(1)
    ring(DOWN, 7)
    ring(UP, 3)
    mixed_theirs(2)
    mixed_theirs(3)
    gate_grad_theirs()
    ring(GATE, 4)
    spread(0)
    spread(1)
    ring(UP, 4)
    for s in range(GROUPS):
        mixed_mine(s)
    gate_grad_mine()
    ring(GATE, 5)
    hand_over(0)
    hand_over(1)
    ring(UP, 5)
    token_theirs(0)
    token_theirs(1)
    ring(GATE, 6)
    conclude(0)
    conclude(1)
    ring(UP, 6)
    token_theirs(2)
    token_theirs(3)
    ring(GATE, 7)
    token_mine(0)
    token_mine(1)
    ring_piece(4, 7)
    spread(2)
    ring_piece(5, 7)
    spread(3)
    token_mine(2)
    token_mine(3)
    spread(4)
    hand_over(2)
    spread(5)
    hand_over(3)
    hand_over(4)
    hand_over(5)
    for p in range(2, PIECES):
        conclude(p)


def output_kernel(mixed, token, ggrad, shares, o_mixed, o_token, o_ggrad, o_gate, o_up, o_down):
    o_mixed[...] = mixed[...]
    o_token[...] = token[...]
    o_ggrad[...] = ggrad[0:o_ggrad.shape[0]]
    o_down[...] = shares[DOWN].astype(F32)
    o_gate[...] = shares[GATE].astype(F32)
    o_up[...] = shares[UP].astype(F32)


def shards(tokens, cotangent, expert_ids, gate_weights, partner, w_gate, w_up, w_down):
    tok_count, model = tokens.shape
    hidden = w_gate.shape[2]
    top = expert_ids.shape[1]
    slots = 8 * (5 * tok_count * top // (4 * 8))
    width = model // RING
    share_rows = width // 4
    piece = hidden // 2
    vmem = pl.BlockSpec(memory_space=pltpu.VMEM)
    hbm = pl.BlockSpec(memory_space=pl.ANY)
    dma = pltpu.SemaphoreType.DMA
    act = pltpu.VMEM((RING, slots, width), BF)
    tok = pltpu.VMEM((RING, tok_count, width), BF)
    small = jax.ShapeDtypeStruct((8, tok_count), F32)
    full = jax.ShapeDtypeStruct((tok_count, model), BF)
    results = pl.pallas_call(
        step_kernel,
        out_shape=[full, full, small, jax.ShapeDtypeStruct((3, share_rows, hidden), BF)],
        in_specs=[pl.BlockSpec(memory_space=pltpu.SMEM)] + [vmem] * 4 + [hbm] * 3,
        out_specs=[vmem] * 4,
        scratch_shapes=[
            pltpu.VMEM((RING, width, hidden), BF),
            pltpu.VMEM((RING, width, hidden), BF),
            pltpu.VMEM((RING, hidden, width), BF),
            pltpu.VMEM((2, tok_count, tok_count), F32),
            pltpu.VMEM((slots, 2 * top * tok_count), BF),
            pltpu.VMEM((2 * top * tok_count, slots), F32),
            pltpu.VMEM((4 * tok_count, slots), BF),
            pltpu.VMEM((2 * tok_count, slots), BF),
            tok, tok,
            pltpu.VMEM((top, tok_count), jnp.int32),
            pltpu.VMEM((top, tok_count), F32),
            act, act, act, act, act, act, act, act,
            tok, tok, tok, tok,
            pltpu.VMEM((8, tok_count), F32),
            pltpu.VMEM((8, tok_count), F32),
            pltpu.VMEM((slots, hidden), F32),
            pltpu.VMEM((slots, hidden), F32),
            pltpu.VMEM((slots, hidden), F32),
            pltpu.VMEM((slots, hidden), BF),
            pltpu.VMEM((slots, hidden), BF),
            pltpu.VMEM((slots, hidden), BF),
            pltpu.VMEM((2 * tok_count, slots), F32),
            pltpu.VMEM((PIECES, RING, 2, 2, share_rows, piece), BF),
            pltpu.VMEM((PIECES, RING, 2, share_rows, piece), BF),
            pltpu.VMEM((PIECES, 2, STEPS, share_rows, piece), BF),
            pltpu.VMEM((PIECES, 2, STEPS, share_rows, piece), BF),
            pltpu.VMEM((PIECES, 2, share_rows, piece), F32),
            pltpu.VMEM((PIECES, 2, share_rows, piece), BF),
            pltpu.VMEM((PIECES, share_rows, piece), BF),
            pltpu.VMEM((PIECES, share_rows, piece), BF),
        ] + [pltpu.VMEM((4, share_rows, piece), BF)] * PIECES + [
            pltpu.VMEM((PIECES, share_rows, piece), BF),
            pltpu.VMEM((PIECES, share_rows, piece), BF),
            dma((3, RING)), dma((4, GROUPS)), dma((4, GROUPS, 3)), dma((4, GROUPS, 3)),
            dma((4, RING)), dma((4, RING)), dma((3,)), dma((3,)),
            dma((PIECES, RING)), dma((PIECES, RING)),
            dma((PIECES, 2, STEPS)), dma((PIECES, 2, STEPS)),
            dma((PIECES,)), dma((PIECES,)),
            dma((PIECES, 3)), dma((PIECES, 3)),
            dma((PIECES,)), dma((PIECES,)),
        ],
        compiler_params=pltpu.CompilerParams(
            collective_id=0, has_side_effects=True, vmem_limit_bytes=67043328
        ),
    )(partner, tokens, cotangent, expert_ids.T, gate_weights.T, w_gate[0], w_up[0], w_down[0])
    grad = jax.ShapeDtypeStruct((share_rows, hidden), F32)
    mixed_out, token_grad, gate_grad, grad_gate, grad_up, grad_down = pl.pallas_call(
        output_kernel,
        out_shape=[full, full, jax.ShapeDtypeStruct((top, tok_count), F32), grad, grad, grad],
        in_specs=[vmem] * 4,
        out_specs=[vmem] * 6,
    )(*results)
    return (mixed_out, token_grad, gate_grad.T, grad_gate[None], grad_up[None], grad_down.T[None])


def solution(mesh):
    in_specs = (
        P(("dp", "expert"), None),
        P(("dp", "expert"), None),
        P(("dp", "expert"), None),
        P(("dp", "expert"), None),
        P(),
        P("expert", None, None),
        P("expert", None, None),
        P("expert", None, None),
    )
    out_specs = (
        P(("dp", "expert"), None),
        P(("dp", "expert"), None),
        P(("dp", "expert"), None),
        P("expert", "dp", None),
        P("expert", "dp", None),
        P("expert", None, "dp"),
    )
    return jax.shard_map(shards, mesh=mesh, in_specs=in_specs, out_specs=out_specs, check_vma=False)
```
